512 devices in a mesh: section: 16 (over x, y_lo, core), expert: 32 (over y_hi, z).
Axes of the slice: x: 4, y: 4 (y_hi: 2, y_lo: 2; y = y_hi * 2 + y_lo), z: 16, core: 2. Of those that a mesh axis runs over, the one named last changes fastest.
Arguments:
- tokens: bfloat16 [16, 2048, 3584], P('section', 'expert'), may hold values from -25 to 25
- norm_gain: bfloat16 [16, 3584], P('section'), may hold values from 0.25 to 1.75
- w_gate: bfloat16 [16, 3584, 4096], P('section', None, 'expert'), may hold values from -0.09375 to 0.09375
- w_up: bfloat16 [16, 3584, 4096], P('section', None, 'expert'), may hold values from -0.09375 to 0.09375
- w_down: bfloat16 [16, 4096, 3584], P('section', 'expert'), may hold values from -0.1875 to 0.1875
- expert_ids: int32 [16, 2048, 2], P('section', 'expert'), may hold values from 0 to 3, as said below
- slot_ids: int32 [16, 2048, 2], P('section', 'expert'), may hold values from 0 to 55, as said below
- route_weight: float32 [16, 2048, 2], P('section', 'expert'), may hold values from 0.2 to 1.2
Outputs:
- next_input: bfloat16 [16, 2048, 3584], P('section', 'expert')
The draws below stay inside these ranges and needn't reach their ends.
Inputs may be any that keep to these rules, and one draw needn't show every extreme that they name: `expert_ids`: each token names 2 different experts. In the rows of one block of 64 tokens (one index of expert in one section) the slots of one expert are 0, 1, 2 and so on in token order, one per token that names it, so the pairs of expert and slot are distinct; one expert, the same in every block, is named by exactly 56 tokens of every block. `slot_ids`: see expert_ids: slots count up from 0 for each expert within the rows of one block.
All inputs are finite; a program needn't handle non-finite values.
Results may differ from the reference program's by a relative error of at most 0.0049.
Values may be sent and summed in bfloat16 or wider, within the bound.
No kernel may reach another device: no remote copies, remote signals or barrier semaphores. Data moves between devices by JAX's collectives and lax.ppermute only.
A program may use at most 128 MiB of HBM per device.

```python
import math
import jax
import jax.numpy as jnp
from jax import lax

D = 3584
H_EXP = 1024
EXPERTS = 4
TOP = 2
TOK_DEV = 64
CAP = 56
SECTIONS = 16
MICRO_TOK = 2048
HID_DEV = 128
N_EXPERT = 32


def routing_tables(key):
    expert_block_list = SECTIONS * (MICRO_TOK // TOK_DEV)
    key_hot, key_off, key_flip, key_swap, key_perm = jax.random.split(jax.random.fold_in(key, 7), 5)
    hot = jax.random.randint(key_hot, (), 0, EXPERTS)
    offsets = jax.random.randint(key_off, (expert_block_list, 1), 0, EXPERTS - 1)
    row_index = jnp.arange(TOK_DEV, dtype=jnp.int32)[None, :]
    is_hot = row_index < CAP
    other_a = (row_index + offsets) % (EXPERTS - 1)
    flips = jax.random.randint(key_flip, (expert_block_list, TOK_DEV), 0, EXPERTS - 2)
    other_b = (other_a + 1 + flips) % (EXPERTS - 1)
    name_a = (hot + 1 + other_a) % EXPERTS
    name_b = (hot + 1 + other_b) % EXPERTS
    first = jnp.where(is_hot, hot, name_a)
    second = jnp.where(is_hot, name_a, name_b)
    swaps = jax.random.randint(key_swap, (expert_block_list, TOK_DEV), 0, 2)
    left = jnp.where(swaps == 1, second, first)
    right = jnp.where(swaps == 1, first, second)
    scores = jax.random.randint(key_perm, (expert_block_list, TOK_DEV), 0, 1 << 20) * TOK_DEV + row_index
    order = jnp.argsort(scores, axis=1)
    left = jnp.take_along_axis(left, order, axis=1)
    right = jnp.take_along_axis(right, order, axis=1)
    pairs = jnp.stack([left, right], axis=-1).astype(jnp.int32)
    equal = (pairs[:, :, :, None] == jnp.arange(EXPERTS, dtype=jnp.int32)).astype(jnp.int32)
    row_has = jnp.sum(equal, axis=2)
    before = jnp.cumsum(row_has, axis=1) - row_has
    slots = jnp.sum(equal * before[:, :, None, :], axis=-1).astype(jnp.int32)
    return (pairs.reshape(SECTIONS, MICRO_TOK, TOP), slots.reshape(SECTIONS, MICRO_TOK, TOP))


def draw_expert_ids(key, part):
    return routing_tables(key)[0]


def draw_slot_ids(key, part):
    return routing_tables(key)[1]


def draw_tokens(key, part):
    key_base, key_row, key_col = jax.random.split(jax.random.fold_in(key, 11), 3)
    shape = (SECTIONS, MICRO_TOK, D)
    row_scale = jnp.exp(jax.random.uniform(key_row, (SECTIONS, MICRO_TOK, 1), jnp.float32, math.log(0.1), 0.0))
    col_scale = jnp.exp(jax.random.uniform(key_col, (SECTIONS, 1, D), jnp.float32, math.log(0.5), math.log(5.0)))
    base = jax.random.truncated_normal(key_base, -4.0, 4.0, shape, jnp.float32)
    return (base * row_scale * col_scale).astype(jnp.bfloat16)


def steps_of(rng, shape, cuts, smallest, top_value):
    level = 1.0
    for axis_at, shards_of in cuts:
        steps = jax.random.uniform(jax.random.fold_in(jax.random.fold_in(rng, 6), axis_at), (shards_of,), jnp.float32, smallest / len(cuts), top_value / len(cuts))
        level = level * jnp.repeat(jnp.exp(steps), shape[axis_at] // shards_of).reshape((-1,) + (1,) * (len(shape) - 1 - axis_at))
    return level


def centred(own_key, extent, deviation, most, cuts=(), kind=jnp.bfloat16):
    entries = deviation * jax.random.normal(own_key, extent, jnp.float32)
    if cuts:
        entries = entries * steps_of(own_key, extent, cuts, -0.22, 0.18)
    return jnp.clip(entries, -most, most).astype(kind)


def setup_inputs(seed: int = 0) -> dict:
    keys = jax.random.split(jax.random.key(seed), 9)
    return {
        "tokens": draw_tokens(jax.random.fold_in(keys[8], 71), 0),
        "norm_gain": jnp.clip(1.0 + 0.15 * jax.random.normal(keys[1], (SECTIONS, D), jnp.float32), 0.25, 1.75).astype(jnp.bfloat16),
        "w_gate": centred(keys[2], (SECTIONS, D, EXPERTS * H_EXP), D ** -0.5, 0.09375, ((0, 16), (2, 32))),
        "w_up": centred(keys[3], (SECTIONS, D, EXPERTS * H_EXP), D ** -0.5, 0.09375, ((0, 16), (2, 32))),
        "w_down": centred(keys[4], (SECTIONS, EXPERTS * H_EXP, D), H_EXP ** -0.5, 0.1875, ((0, 16), (1, 32))),
        "expert_ids": draw_expert_ids(jax.random.fold_in(keys[8], 71), 0),
        "slot_ids": draw_slot_ids(jax.random.fold_in(keys[8], 71), 0),
        "route_weight": jnp.clip(0.2 + 1 * jax.random.uniform(keys[7], (SECTIONS, MICRO_TOK, TOP), jnp.float32) ** steps_of(keys[7], (SECTIONS, MICRO_TOK, TOP), ((0, 16), (1, 32)), -0.2, 0.2), 0.2, 1.2),
    }


def rms_normed(tokens, gain):
    values = tokens.astype(jnp.float32)
    mean_sq = lax.optimization_barrier(jnp.mean(values * values, axis=-1, keepdims=True))
    return (values * lax.rsqrt(mean_sq + 1e-06) * gain.astype(jnp.float32)).astype(jnp.bfloat16)

def section_layer(operands):
    tokens, gain, w_gate, w_up, w_down, expert_ids, slot_ids, route_weight = operands
    normed = rms_normed(tokens, gain)
    expert_block_list = normed.reshape(N_EXPERT, TOK_DEV, D).astype(jnp.float32)
    codes = (expert_ids * CAP + slot_ids).reshape(N_EXPERT, TOK_DEV, TOP)
    columns = jnp.arange(EXPERTS * CAP, dtype=jnp.int32)
    expert_match_mask = codes[:, :, :, None] == columns
    expert_selector_index = lax.optimization_barrier(jnp.sum(expert_match_mask.astype(jnp.float32), axis=2))
    routed_token_rows = jnp.einsum('yhi,yhe->yie', expert_selector_index, expert_block_list).astype(jnp.bfloat16)
    routed_token_rows = routed_token_rows.reshape(N_EXPERT, EXPERTS, CAP, D)
    groups = H_EXP // HID_DEV

    def one_expert(expert):
        rows = lax.dynamic_index_in_dim(routed_token_rows, expert, 1, keepdims=False).reshape(N_EXPERT * CAP, D)
        gate_weight_columns = lax.dynamic_slice_in_dim(w_gate, expert * H_EXP, H_EXP, 1)
        up_cols = lax.dynamic_slice_in_dim(w_up, expert * H_EXP, H_EXP, 1)
        down_rows = lax.dynamic_slice_in_dim(w_down, expert * H_EXP, H_EXP, 0)
        gate_part = jnp.dot(rows, gate_weight_columns, preferred_element_type=jnp.float32)
        up_part = jnp.dot(rows, up_cols, preferred_element_type=jnp.float32)
        hidden = (jax.nn.silu(gate_part) * up_part).astype(jnp.bfloat16)
        pieces = jnp.einsum('rgh,ghd->grd', hidden.reshape(N_EXPERT * CAP, groups, HID_DEV).astype(jnp.float32), down_rows.reshape(groups, HID_DEV, D).astype(jnp.float32))
        rounded = lax.optimization_barrier(pieces.astype(jnp.bfloat16))
        return lax.optimization_barrier(jnp.sum(rounded.astype(jnp.float32), axis=0)).reshape(N_EXPERT, CAP, D)
    expert_out = lax.map(one_expert, jnp.arange(EXPERTS, dtype=jnp.int32))
    sorted_token_rows = jnp.transpose(expert_out, (1, 0, 2, 3)).reshape(N_EXPERT, EXPERTS * CAP, D)
    weights = route_weight.reshape(N_EXPERT, TOK_DEV, TOP)[:, :, :, None]
    gate_mixing_weight = lax.optimization_barrier(jnp.sum(jnp.where(expert_match_mask, weights, jnp.zeros_like(weights)), axis=2))
    residual_branch = jnp.einsum('uym,umh->uyh', gate_mixing_weight, sorted_token_rows, precision=lax.Precision.HIGHEST)
    return (tokens.astype(jnp.float32) + residual_branch.reshape(MICRO_TOK, D)).astype(jnp.bfloat16)

def reference(tokens, norm_gain, w_gate, w_up, w_down, expert_ids, slot_ids, route_weight):
    mixed = lax.map(section_layer, (tokens, norm_gain, w_gate, w_up, w_down, expert_ids, slot_ids, route_weight))
    return jnp.roll(mixed, 1, axis=0)
```

```python
import jax
import jax.numpy as jnp
from jax import lax
from jax.sharding import Mesh
from jax.sharding import PartitionSpec as P

EXPERTS = 4


def local(tokens, norm_gain, w_gate, w_up, w_down, expert_ids, slot_ids, route_weight):
    row, col = lax.axis_index("row"), lax.axis_index("col")
    rows, cols = lax.axis_size("row"), lax.axis_size("col")
    count, width = tokens.shape[1:]
    swap = [(0, 1), (1, 0)]

    named = expert_ids[0][None] == jnp.arange(EXPERTS, dtype=jnp.int32)[:, None, None]
    dense = jnp.sum(jnp.where(named, route_weight[0][None], 0.0), axis=2)
    spread = jnp.broadcast_to(dense.reshape(1, -1), (cols, EXPERTS * count))
    spread = lax.all_to_all(spread, "col", split_axis=0, concat_axis=0, tiled=True)
    spread = spread.reshape(cols, EXPERTS, count)

    values = tokens[0].astype(jnp.float32)
    mean_sq = jnp.mean(values * values, axis=-1, keepdims=True)
    normed = values * lax.rsqrt(mean_sq + 1e-06) * norm_gain[0].astype(jnp.float32)
    gathered = lax.all_gather(normed.astype(jnp.bfloat16), "col", axis=0, tiled=True)

    gate_far = lax.ppermute(w_gate[0], "row", swap)
    up_far = lax.ppermute(w_up[0], "row", swap)
    down_far = lax.ppermute(w_down[0], "row", swap)
    first = jnp.concatenate([w_gate[0], gate_far, w_up[0], up_far], axis=1)
    second = jnp.concatenate([w_down[0], down_far], axis=0)
    per_row = EXPERTS // rows
    mine = col // (cols // per_row)

    def weight_of(expert):
        picked = lax.dynamic_index_in_dim(spread, expert, 1, keepdims=False)
        return jnp.broadcast_to(picked.reshape(-1, 1), (cols * count, w_gate.shape[2]))

    weights = jnp.concatenate(
        [weight_of(row * per_row + mine), weight_of((1 - row) * per_row + mine)], axis=1
    )
    both = jnp.dot(gathered, first, preferred_element_type=jnp.float32)
    half = both.shape[1] // 2
    hidden = (jax.nn.silu(both[:, :half]) * both[:, half:] * weights).astype(jnp.bfloat16)
    piece = jnp.dot(hidden, second, preferred_element_type=jnp.float32).astype(jnp.bfloat16)
    summed = lax.psum_scatter(piece, "col", scatter_dimension=0, tiled=True)
    mixed = (values + summed.astype(jnp.float32)).astype(jnp.bfloat16)[None]
    sections = lax.axis_size("section")
    return lax.ppermute(mixed, "section", [(i, (i + 1) % sections) for i in range(sections)])


def solution(mesh):
    sections, members = mesh.devices.shape
    fine = Mesh(mesh.devices.reshape(sections, 2, members // 2), ("section", "row", "col"))
    split = ("row", "col")
    placed = (
        P("section", split, None),
        P("section", None),
        P("section", None, split),
        P("section", None, split),
        P("section", split, None),
        P("section", split, None),
        P("section", split, None),
        P("section", split, None),
    )
    return jax.shard_map(
        local, mesh=fine, in_specs=placed, out_specs=P("section", split, None), check_vma=False
    )
```

```python
import jax
import jax.numpy as jnp
from jax import lax
from jax.sharding import Mesh
from jax.sharding import PartitionSpec as P

EXPERTS = 4


def shift(value, steps, ahead=0):
    sections, cols = lax.axis_size("section"), lax.axis_size("col")
    if not ahead:
        return lax.ppermute(value, "col", [(i, (i + steps) % cols) for i in range(cols)])
    pairs = [
        (s * cols + i, (s + ahead) % sections * cols + (i + steps) % cols)
        for s in range(sections)
        for i in range(cols)
    ]
    return lax.ppermute(value, ("section", "col"), pairs)


def local(tokens, norm_gain, w_gate, w_up, w_down, expert_ids, slot_ids, route_weight):
    row, col = lax.axis_index("row"), lax.axis_index("col")
    rows, cols = lax.axis_size("row"), lax.axis_size("col")
    count, width = tokens.shape[1:]
    units = w_gate.shape[2]
    far, part = cols // 2, count // 2
    swap = [(0, 1), (1, 0)]

    values = tokens[0].astype(jnp.float32)
    mean_sq = jnp.mean(values * values, axis=-1, keepdims=True)
    normed = values * lax.rsqrt(mean_sq + 1e-06) * norm_gain[0].astype(jnp.float32)
    normed = normed.astype(jnp.bfloat16)

    behind, before = [normed], [normed]
    for s in range(1, far):
        behind.append(shift(behind[-1], 1))
        before.append(shift(before[-1], -1))
    opposite = jnp.concatenate(
        [shift(behind[-1][:part], 1), shift(before[-1][part:], -1)], axis=0
    )

    gate_far = lax.ppermute(w_gate[0], "row", swap)
    up_far = lax.ppermute(w_up[0], "row", swap)
    down_far = lax.ppermute(w_down[0], "row", swap)
    first = jnp.concatenate([w_gate[0], gate_far, w_up[0], up_far], axis=1)
    second = jnp.concatenate([w_down[0], down_far], axis=0)
    first, second = lax.optimization_barrier((first, second))

    named = expert_ids[0][None] == jnp.arange(EXPERTS, dtype=jnp.int32)[:, None, None]
    dense = jnp.sum(jnp.where(named, route_weight[0][None], 0.0), axis=2)
    spread = jnp.broadcast_to(dense.reshape(1, -1), (cols, EXPERTS * count))
    spread = lax.all_to_all(spread, "col", split_axis=0, concat_axis=0, tiled=True)
    spread = spread.reshape(cols, EXPERTS, count)
    spread = lax.dynamic_slice_in_dim(jnp.concatenate([spread, spread]), col, cols, 0)
    per_row = EXPERTS // rows
    mine = col // (cols // per_row)

    def weight_of(expert):
        picked = lax.dynamic_index_in_dim(spread, expert, 1, keepdims=False)
        return jnp.broadcast_to(picked.reshape(-1, 1), (cols * count, units))

    weights = lax.optimization_barrier(
        jnp.concatenate(
            [weight_of(row * per_row + mine), weight_of((1 - row) * per_row + mine)], axis=1
        )
    )

    def weight_rows(offset):
        start = offset % cols * count
        return weights[start : start + count]

    def expert_sums(block, weight):
        both = jnp.dot(block, first, preferred_element_type=jnp.float32)
        half = both.shape[1] // 2
        hidden = (jax.nn.silu(both[:, :half]) * both[:, half:] * weight).astype(jnp.bfloat16)
        return lax.optimization_barrier(
            jnp.dot(hidden, second, preferred_element_type=jnp.float32)
        )

    piece = expert_sums(opposite, weight_rows(far)).astype(jnp.bfloat16)
    left, right = shift(piece[:part], -1), shift(piece[part:], 1)
    for s in range(far - 1, 0, -1):
        pair = jnp.concatenate([behind[s], before[s]], axis=0)
        weight = jnp.concatenate([weight_rows(-s), weight_rows(s)], axis=0)
        sums = expert_sums(pair, weight)
        to_left, to_right = sums[:count], sums[count:]
        if s == far - 1:
            to_left = jnp.concatenate(
                [to_left[:part] + left.astype(jnp.float32), to_left[part:]], axis=0
            )
            to_right = jnp.concatenate(
                [to_right[:part], to_right[part:] + right.astype(jnp.float32)], axis=0
            )
        else:
            to_left = to_left + left.astype(jnp.float32)
            to_right = to_right + right.astype(jnp.float32)
        ahead = 1 if s == 1 else 0
        left = shift(to_left.astype(jnp.bfloat16), -1, ahead)
        right = shift(to_right.astype(jnp.bfloat16), 1, ahead)

    own = shift(expert_sums(normed, weight_rows(0)).astype(jnp.bfloat16), 0, 1)
    kept = shift(tokens[0], 0, 1).astype(jnp.float32) + own.astype(jnp.float32)
    mixed = kept + left.astype(jnp.float32) + right.astype(jnp.float32)
    return mixed.astype(jnp.bfloat16)[None]


def solution(mesh):
    sections, members = mesh.devices.shape
    fine = Mesh(mesh.devices.reshape(sections, 2, members // 2), ("section", "row", "col"))
    split = ("row", "col")
    placed = (
        P("section", split, None),
        P("section", None),
        P("section", None, split),
        P("section", None, split),
        P("section", split, None),
        P("section", split, None),
        P("section", split, None),
        P("section", split, None),
    )
    return jax.shard_map(
        local, mesh=fine, in_specs=placed, out_specs=P("section", split, None), check_vma=False
    )
```

```python
import jax
import jax.numpy as jnp
from jax import lax
from jax.sharding import Mesh
from jax.sharding import PartitionSpec as P

EXPERTS = 4
PARTS = 3
LANES = 128


def shift(value, steps, ahead=0):
    sections, cols = lax.axis_size("section"), lax.axis_size("col")
    if not ahead:
        return lax.ppermute(value, "col", [(i, (i + steps) % cols) for i in range(cols)])
    pairs = [
        (s * cols + i, (s + ahead) % sections * cols + (i + steps) % cols)
        for s in range(sections)
        for i in range(cols)
    ]
    return lax.ppermute(value, ("section", "col"), pairs)


def across(value):
    return lax.ppermute(value, "row", [(0, 1), (1, 0)])


def rounded(value):
    return lax.reduce_precision(value, 8, 7)


def local(tokens, norm_gain, w_gate, w_up, w_down, expert_ids, slot_ids, route_weight):
    return layer(tokens, norm_gain, w_gate, w_up, w_down, expert_ids, route_weight)


def layer(tokens, norm_gain, w_gate, w_up, w_down, expert_ids, route_weight):
    row, col = lax.axis_index("row"), lax.axis_index("col")
    rows, cols = lax.axis_size("row"), lax.axis_size("col")
    count, width = tokens.shape[1:]
    units = w_gate.shape[2]
    far, part = cols // 2, count // 2

    values = tokens[0].astype(jnp.float32)
    mean_sq = jnp.mean(values * values, axis=-1, keepdims=True)
    normed = values * lax.rsqrt(mean_sq + 1e-06) * norm_gain[0].astype(jnp.float32)

    lane = jnp.arange(LANES, dtype=jnp.int32)[None]
    ids, route = expert_ids[0], route_weight[0]
    dense = jnp.zeros((count, LANES), jnp.float32)
    for k in range(ids.shape[1]):
        dense = dense + jnp.where(ids[:, k : k + 1] == lane % EXPERTS, route[:, k : k + 1], 0.0)
    high = rounded(dense)
    middle = rounded(dense - high)
    low = dense - high - middle
    level = lane // EXPERTS
    parts = jnp.where(level == 0, high, jnp.where(level == 1, middle, low))
    parts = jnp.where(level < PARTS, parts, 0.0)
    block = jnp.concatenate([normed.astype(jnp.bfloat16), parts.astype(jnp.bfloat16)], axis=1)

    behind, before = [block], [block]
    for _ in range(1, far):
        behind.append(shift(behind[-1], 1))
        before.append(shift(before[-1], -1))
    opposite = jnp.concatenate([shift(behind[-1][:part], 1), shift(before[-1][part:], -1)], axis=0)

    gate_far = across(w_gate[0])
    up_far = across(w_up[0])
    down_far = across(w_down[0])
    first = jnp.concatenate([w_gate[0], gate_far, w_up[0], up_far], axis=1)
    second = jnp.concatenate([w_down[0], down_far], axis=0)
    first, second = lax.optimization_barrier((first, second))

    per_row = EXPERTS // rows
    mine = col // (cols // per_row)
    near_expert, far_expert = row * per_row + mine, (1 - row) * per_row + mine
    unit = jnp.arange(2 * units, dtype=jnp.int32)[None]
    wanted = jnp.where(unit < units, near_expert, far_expert)
    pick = lax.optimization_barrier((lane.T % EXPERTS == wanted).astype(jnp.bfloat16))

    def expert_sums(block):
        weight = jnp.dot(block[:, width:], pick, preferred_element_type=jnp.float32)
        both = jnp.dot(block[:, :width], first, preferred_element_type=jnp.float32)
        half = both.shape[1] // 2
        hidden = (jax.nn.silu(both[:, :half]) * both[:, half:] * weight).astype(jnp.bfloat16)
        return lax.optimization_barrier(
            jnp.dot(hidden, second, preferred_element_type=jnp.float32)
        )

    piece = expert_sums(opposite).astype(jnp.bfloat16)
    left, right = shift(piece[:part], -1), shift(piece[part:], 1)
    for s in range(far - 1, 0, -1):
        to_left, to_right = expert_sums(behind[s]), expert_sums(before[s])
        if s == far - 1:
            to_left = jnp.concatenate(
                [to_left[:part] + left.astype(jnp.float32), to_left[part:]], axis=0
            )
            to_right = jnp.concatenate(
                [to_right[:part], to_right[part:] + right.astype(jnp.float32)], axis=0
            )
        else:
            to_left = to_left + left.astype(jnp.float32)
            to_right = to_right + right.astype(jnp.float32)
        ahead = 1 if s == 1 else 0
        left = shift(to_left.astype(jnp.bfloat16), -1, ahead)
        right = shift(to_right.astype(jnp.bfloat16), 1, ahead)

    own = shift(expert_sums(block).astype(jnp.bfloat16), 0, 1)
    kept = shift(tokens[0], 0, 1).astype(jnp.float32) + own.astype(jnp.float32)
    mixed = kept + left.astype(jnp.float32) + right.astype(jnp.float32)
    return mixed.astype(jnp.bfloat16)[None]


def solution(mesh):
    sections, members = mesh.devices.shape
    fine = Mesh(mesh.devices.reshape(sections, 2, members // 2), ("section", "row", "col"))
    split = ("row", "col")
    placed = (
        P("section", split, None),
        P("section", None),
        P("section", None, split),
        P("section", None, split),
        P("section", split, None),
        P("section", split, None),
        P("section", split, None),
        P("section", split, None),
    )
    return jax.shard_map(
        local, mesh=fine, in_specs=placed, out_specs=P("section", split, None), check_vma=False
    )
```

```python
import jax
import jax.numpy as jnp
from jax import lax
from jax.experimental import pallas as pl
from jax.experimental.pallas import tpu as pltpu
from jax.sharding import Mesh
from jax.sharding import PartitionSpec as P

EXPERTS = 4
ROW_TILE = 256
COLUMN_TILE = 512


def norm_kernel(token_ref, gain_ref, out_ref):
    values = token_ref[...].astype(jnp.float32)
    mean_sq = jnp.mean(values * values, axis=-1, keepdims=True)
    scale = lax.rsqrt(mean_sq + 1e-06)
    out_ref[...] = (values * scale * gain_ref[...].astype(jnp.float32)).astype(out_ref.dtype)


def normalise(tokens, gain):
    return pl.pallas_call(
        norm_kernel,
        out_shape=jax.ShapeDtypeStruct(tokens.shape, tokens.dtype),
        in_specs=[pl.BlockSpec(memory_space=pltpu.VMEM)] * 2,
        out_specs=pl.BlockSpec(memory_space=pltpu.VMEM),
        name="normalise",
    )(tokens, gain)


def expert_kernel(row_ref, near_ref, far_ref, first_ref, second_ref, out_ref, w1, w2, sems):
    copies = (
        pltpu.make_async_copy(first_ref, w1, sems.at[0]),
        pltpu.make_async_copy(second_ref, w2, sems.at[1]),
    )

    @pl.when(pl.program_id(0) == 0)
    def _():
        for copy in copies:
            copy.start()
        copies[0].wait()

    both = jnp.dot(row_ref[...], w1[...], preferred_element_type=jnp.float32)
    half, units = both.shape[1] // 2, near_ref.shape[1]
    gate, up = both[:, :half], both[:, half:]
    hidden = gate / (1.0 + jnp.exp(-gate)) * up
    hidden = jnp.concatenate(
        [hidden[:, :units] * near_ref[...], hidden[:, units:] * far_ref[...]], axis=1
    ).astype(jnp.bfloat16)

    @pl.when(pl.program_id(0) == 0)
    def _():
        copies[1].wait()

    for at in range(0, out_ref.shape[1], COLUMN_TILE):
        span = slice(at, at + COLUMN_TILE)
        piece = jnp.dot(hidden, w2[:, span], preferred_element_type=jnp.float32)
        out_ref[:, span] = piece.astype(out_ref.dtype)


def expert_sums(gathered, near, far, first, second):
    count, width = gathered.shape
    tile = min(ROW_TILE, count)

    def tiled(columns):
        return pl.BlockSpec((tile, columns), lambda i: (i, 0))

    return pl.pallas_call(
        expert_kernel,
        grid=(count // tile,),
        out_shape=jax.ShapeDtypeStruct(gathered.shape, gathered.dtype),
        in_specs=[
            tiled(width),
            tiled(near.shape[1]),
            tiled(far.shape[1]),
            pl.BlockSpec(memory_space=pl.ANY),
            pl.BlockSpec(memory_space=pl.ANY),
        ],
        out_specs=tiled(width),
        scratch_shapes=[
            pltpu.VMEM(first.shape, first.dtype),
            pltpu.VMEM(second.shape, second.dtype),
            pltpu.SemaphoreType.DMA((2,)),
        ],
        compiler_params=pltpu.CompilerParams(vmem_limit_bytes=58 * 1024 * 1024),
        cost_estimate=pl.CostEstimate(
            flops=2 * count * (first.size + second.size),
            bytes_accessed=2 * gathered.size * 2,
            transcendentals=count * first.shape[1] // 2,
        ),
        name="expert_sums",
    )(gathered, near, far, first, second)


def onward(value):
    sections = lax.axis_size("section")
    return lax.ppermute(value, "section", [(i, (i + 1) % sections) for i in range(sections)])


def local(tokens, norm_gain, w_gate, w_up, w_down, expert_ids, slot_ids, route_weight):
    row, col = lax.axis_index("row"), lax.axis_index("col")
    rows, cols = lax.axis_size("row"), lax.axis_size("col")
    count = tokens.shape[1]
    swap = [(0, 1), (1, 0)]

    named = expert_ids[0][None] == jnp.arange(EXPERTS, dtype=jnp.int32)[:, None, None]
    dense = jnp.sum(jnp.where(named, route_weight[0][None], 0.0), axis=2)
    spread = jnp.broadcast_to(dense.reshape(1, -1), (cols, EXPERTS * count))
    spread = lax.all_to_all(spread, "col", split_axis=0, concat_axis=0, tiled=True)
    spread = spread.reshape(cols, EXPERTS, count)

    normed = normalise(tokens[0], norm_gain)
    gathered = lax.all_gather(normed, "col", axis=0, tiled=True)

    gate_far = lax.ppermute(w_gate[0], "row", swap)
    up_far = lax.ppermute(w_up[0], "row", swap)
    down_far = lax.ppermute(w_down[0], "row", swap)
    first = jnp.concatenate([w_gate[0], gate_far, w_up[0], up_far], axis=1)
    second = jnp.concatenate([w_down[0], down_far], axis=0)
    per_row = EXPERTS // rows
    mine = col // (cols // per_row)

    def weight_of(expert):
        picked = lax.dynamic_index_in_dim(spread, expert, 1, keepdims=False)
        return jnp.broadcast_to(picked.reshape(-1, 1), (cols * count, w_gate.shape[2]))

    near, far = weight_of(row * per_row + mine), weight_of((1 - row) * per_row + mine)
    first, second, near, far = lax.optimization_barrier((first, second, near, far))
    piece = expert_sums(gathered, near, far, first, second)
    summed = lax.psum_scatter(piece, "col", scatter_dimension=0, tiled=True)
    mixed = onward(tokens[0]).astype(jnp.float32) + onward(summed).astype(jnp.float32)
    return mixed.astype(jnp.bfloat16)[None]


def solution(mesh):
    sections, members = mesh.devices.shape
    fine = Mesh(mesh.devices.reshape(sections, 2, members // 2), ("section", "row", "col"))
    split = ("row", "col")
    placed = (
        P("section", split, None),
        P("section", None),
        P("section", None, split),
        P("section", None, split),
        P("section", split, None),
        P("section", split, None),
        P("section", split, None),
        P("section", split, None),
    )
    return jax.shard_map(
        local, mesh=fine, in_specs=placed, out_specs=P("section", split, None), check_vma=False
    )
```

```python
import jax
import jax.numpy as jnp
from jax import lax
from jax.experimental import pallas as pl
from jax.experimental.pallas import tpu as pltpu
from jax.sharding import Mesh
from jax.sharding import PartitionSpec as P

EXPERTS = 4
ROW_TILE = 128
COLUMN_TILE = 512


def norm_kernel(token_ref, gain_ref, out_ref):
    values = token_ref[...].astype(jnp.float32)
    mean_sq = jnp.mean(values * values, axis=-1, keepdims=True)
    scale = lax.rsqrt(mean_sq + 1e-06)
    out_ref[...] = (values * scale * gain_ref[...].astype(jnp.float32)).astype(out_ref.dtype)


def normalise(tokens, gain):
    return pl.pallas_call(
        norm_kernel,
        out_shape=jax.ShapeDtypeStruct(tokens.shape, tokens.dtype),
        in_specs=[pl.BlockSpec(memory_space=pltpu.VMEM)] * 2,
        out_specs=pl.BlockSpec(memory_space=pltpu.VMEM),
        name="normalise",
    )(tokens, gain)


def expert_kernel(row_ref, near_ref, far_ref, first_ref, second_ref, out_ref, w1, w2, sems):
    copies = (
        pltpu.make_async_copy(first_ref, w1, sems.at[0]),
        pltpu.make_async_copy(second_ref, w2, sems.at[1]),
    )

    @pl.when(pl.program_id(0) == 0)
    def _():
        for copy in copies:
            copy.start()
        copies[0].wait()

    both = jnp.dot(row_ref[...], w1[...], preferred_element_type=jnp.float32)
    half, units = both.shape[1] // 2, near_ref.shape[1]
    gate, up = both[:, :half], both[:, half:]
    hidden = gate / (1.0 + jnp.exp(-gate)) * up
    hidden = jnp.concatenate(
        [hidden[:, :units] * near_ref[...], hidden[:, units:] * far_ref[...]], axis=1
    ).astype(jnp.bfloat16)

    @pl.when(pl.program_id(0) == 0)
    def _():
        copies[1].wait()

    for at in range(0, out_ref.shape[1], COLUMN_TILE):
        span = slice(at, at + COLUMN_TILE)
        piece = jnp.dot(hidden, w2[:, span], preferred_element_type=jnp.float32)
        out_ref[:, span] = piece.astype(out_ref.dtype)


def expert_sums(gathered, near, far, first, second):
    count, width = gathered.shape
    tile = min(ROW_TILE, count)

    def tiled(columns):
        return pl.BlockSpec((tile, columns), lambda i: (i, 0))

    return pl.pallas_call(
        expert_kernel,
        grid=(count // tile,),
        out_shape=jax.ShapeDtypeStruct(gathered.shape, gathered.dtype),
        in_specs=[
            tiled(width),
            tiled(near.shape[1]),
            tiled(far.shape[1]),
            pl.BlockSpec(memory_space=pl.ANY),
            pl.BlockSpec(memory_space=pl.ANY),
        ],
        out_specs=tiled(width),
        scratch_shapes=[
            pltpu.VMEM(first.shape, first.dtype),
            pltpu.VMEM(second.shape, second.dtype),
            pltpu.SemaphoreType.DMA((2,)),
        ],
        compiler_params=pltpu.CompilerParams(vmem_limit_bytes=58 * 1024 * 1024),
        cost_estimate=pl.CostEstimate(
            flops=2 * count * (first.size + second.size),
            bytes_accessed=2 * gathered.size * 2,
            transcendentals=count * first.shape[1] // 2,
        ),
        name="expert_sums",
    )(gathered, near, far, first, second)


def onward(value):
    sections = lax.axis_size("section")
    return lax.ppermute(value, "section", [(i, (i + 1) % sections) for i in range(sections)])


def local(tokens, norm_gain, w_gate, w_up, w_down, expert_ids, slot_ids, route_weight):
    row, col = lax.axis_index("row"), lax.axis_index("col")
    rows, cols = lax.axis_size("row"), lax.axis_size("col")
    count = tokens.shape[1]
    swap = [(0, 1), (1, 0)]

    named = expert_ids[0][None] == jnp.arange(EXPERTS, dtype=jnp.int32)[:, None, None]
    dense = jnp.sum(jnp.where(named, route_weight[0][None], 0.0), axis=2)
    spread = jnp.broadcast_to(dense.reshape(1, -1), (cols, EXPERTS * count))
    spread = lax.all_to_all(spread, "col", split_axis=0, concat_axis=0, tiled=True)
    spread = spread.reshape(cols, EXPERTS, count)

    normed = normalise(tokens[0], norm_gain)
    gathered = lax.all_gather(normed, "col", axis=0, tiled=True)

    gate_far = lax.ppermute(w_gate[0], "row", swap)
    up_far = lax.ppermute(w_up[0], "row", swap)
    down_far = lax.ppermute(w_down[0], "row", swap)
    first = jnp.concatenate([w_gate[0], gate_far, w_up[0], up_far], axis=1)
    second = jnp.concatenate([w_down[0], down_far], axis=0)
    per_row = EXPERTS // rows
    mine = col // (cols // per_row)

    def weight_of(expert):
        picked = lax.dynamic_index_in_dim(spread, expert, 1, keepdims=False)
        return jnp.broadcast_to(picked.reshape(-1, 1), (cols * count, w_gate.shape[2]))

    near, far = weight_of(row * per_row + mine), weight_of((1 - row) * per_row + mine)
    first, second, near, far = lax.optimization_barrier((first, second, near, far))
    piece = expert_sums(gathered, near, far, first, second)
    summed = lax.psum_scatter(piece, "col", scatter_dimension=0, tiled=True)
    mixed = onward(tokens[0]).astype(jnp.float32) + onward(summed).astype(jnp.float32)
    return mixed.astype(jnp.bfloat16)[None]


def solution(mesh):
    sections, members = mesh.devices.shape
    fine = Mesh(mesh.devices.reshape(sections, 2, members // 2), ("section", "row", "col"))
    split = ("row", "col")
    placed = (
        P("section", split, None),
        P("section", None),
        P("section", None, split),
        P("section", None, split),
        P("section", split, None),
        P("section", split, None),
        P("section", split, None),
        P("section", split, None),
    )
    return jax.shard_map(
        local, mesh=fine, in_specs=placed, out_specs=P("section", split, None), check_vma=False
    )
```

```python
import jax
import jax.numpy as jnp
from jax import lax
from jax.experimental import pallas as pl
from jax.experimental.pallas import tpu as pltpu
from jax.sharding import Mesh
from jax.sharding import PartitionSpec as P

EXPERTS = 4
ROW_TILE = 512
COLUMN_TILE = 512


def norm_kernel(token_ref, gain_ref, out_ref):
    values = token_ref[...].astype(jnp.float32)
    mean_sq = jnp.mean(values * values, axis=-1, keepdims=True)
    scale = lax.rsqrt(mean_sq + 1e-06)
    out_ref[...] = (values * scale * gain_ref[...].astype(jnp.float32)).astype(out_ref.dtype)


def normalise(tokens, gain):
    return pl.pallas_call(
        norm_kernel,
        out_shape=jax.ShapeDtypeStruct(tokens.shape, tokens.dtype),
        in_specs=[pl.BlockSpec(memory_space=pltpu.VMEM)] * 2,
        out_specs=pl.BlockSpec(memory_space=pltpu.VMEM),
        name="normalise",
    )(tokens, gain)


def expert_kernel(row_ref, near_ref, far_ref, first_ref, second_ref, out_ref, w1, w2, sems):
    copies = (
        pltpu.make_async_copy(first_ref, w1, sems.at[0]),
        pltpu.make_async_copy(second_ref, w2, sems.at[1]),
    )

    @pl.when(pl.program_id(0) == 0)
    def _():
        for copy in copies:
            copy.start()
        for copy in copies:
            copy.wait()

    both = jnp.dot(row_ref[...], w1[...], preferred_element_type=jnp.float32)
    half, units = both.shape[1] // 2, near_ref.shape[1]
    gate, up = both[:, :half], both[:, half:]
    hidden = gate / (1.0 + jnp.exp(-gate)) * up
    hidden = jnp.concatenate(
        [hidden[:, :units] * near_ref[...], hidden[:, units:] * far_ref[...]], axis=1
    ).astype(jnp.bfloat16)

    for at in range(0, out_ref.shape[1], COLUMN_TILE):
        span = slice(at, at + COLUMN_TILE)
        piece = jnp.dot(hidden, w2[:, span], preferred_element_type=jnp.float32)
        out_ref[:, span] = piece.astype(out_ref.dtype)


def expert_sums(gathered, near, far, first, second):
    count, width = gathered.shape
    tile = min(ROW_TILE, count)

    def tiled(columns):
        return pl.BlockSpec((tile, columns), lambda i: (i, 0))

    return pl.pallas_call(
        expert_kernel,
        grid=(count // tile,),
        out_shape=jax.ShapeDtypeStruct(gathered.shape, gathered.dtype),
        in_specs=[
            tiled(width),
            tiled(near.shape[1]),
            tiled(far.shape[1]),
            pl.BlockSpec(memory_space=pl.ANY),
            pl.BlockSpec(memory_space=pl.ANY),
        ],
        out_specs=tiled(width),
        scratch_shapes=[
            pltpu.VMEM(first.shape, first.dtype),
            pltpu.VMEM(second.shape, second.dtype),
            pltpu.SemaphoreType.DMA((2,)),
        ],
        compiler_params=pltpu.CompilerParams(vmem_limit_bytes=58 * 1024 * 1024),
        cost_estimate=pl.CostEstimate(
            flops=2 * count * (first.size + second.size),
            bytes_accessed=2 * gathered.size * 2,
            transcendentals=count * first.shape[1] // 2,
        ),
        name="expert_sums",
    )(gathered, near, far, first, second)


def onward(value):
    sections = lax.axis_size("section")
    return lax.ppermute(value, "section", [(i, (i + 1) % sections) for i in range(sections)])


def local(tokens, norm_gain, w_gate, w_up, w_down, expert_ids, slot_ids, route_weight):
    row, col = lax.axis_index("row"), lax.axis_index("col")
    rows, cols = lax.axis_size("row"), lax.axis_size("col")
    count = tokens.shape[1]
    swap = [(0, 1), (1, 0)]

    named = expert_ids[0][None] == jnp.arange(EXPERTS, dtype=jnp.int32)[:, None, None]
    dense = jnp.sum(jnp.where(named, route_weight[0][None], 0.0), axis=2)
    spread = jnp.broadcast_to(dense.reshape(1, -1), (cols, EXPERTS * count))
    spread = lax.all_to_all(spread, "col", split_axis=0, concat_axis=0, tiled=True)
    spread = spread.reshape(cols, EXPERTS, count)

    normed = normalise(tokens[0], norm_gain)
    gathered = lax.all_gather(normed, "col", axis=0, tiled=True)

    gate_far = lax.ppermute(w_gate[0], "row", swap)
    up_far = lax.ppermute(w_up[0], "row", swap)
    down_far = lax.ppermute(w_down[0], "row", swap)
    first = jnp.concatenate([w_gate[0], gate_far, w_up[0], up_far], axis=1)
    second = jnp.concatenate([w_down[0], down_far], axis=0)
    per_row = EXPERTS // rows
    mine = col // (cols // per_row)

    def weight_of(expert):
        picked = lax.dynamic_index_in_dim(spread, expert, 1, keepdims=False)
        return jnp.broadcast_to(picked.reshape(-1, 1), (cols * count, w_gate.shape[2]))

    near, far = weight_of(row * per_row + mine), weight_of((1 - row) * per_row + mine)
    first, second, near, far = lax.optimization_barrier((first, second, near, far))
    piece = expert_sums(gathered, near, far, first, second)
    summed = lax.psum_scatter(piece, "col", scatter_dimension=0, tiled=True)
    mixed = onward(tokens[0]).astype(jnp.float32) + onward(summed).astype(jnp.float32)
    return mixed.astype(jnp.bfloat16)[None]


def solution(mesh):
    sections, members = mesh.devices.shape
    fine = Mesh(mesh.devices.reshape(sections, 2, members // 2), ("section", "row", "col"))
    split = ("row", "col")
    placed = (
        P("section", split, None),
        P("section", None),
        P("section", None, split),
        P("section", None, split),
        P("section", split, None),
        P("section", split, None),
        P("section", split, None),
        P("section", split, None),
    )
    return jax.shard_map(
        local, mesh=fine, in_specs=placed, out_specs=P("section", split, None), check_vma=False
    )
```

```python
import jax
import jax.numpy as jnp
from jax import lax
from jax.experimental import pallas as pl
from jax.experimental.pallas import tpu as pltpu
from jax.sharding import Mesh
from jax.sharding import PartitionSpec as P

EXPERTS = 4


def norm_kernel(token_ref, gain_ref, out_ref):
    values = token_ref[...].astype(jnp.float32)
    mean_sq = jnp.mean(values * values, axis=-1, keepdims=True)
    scale = lax.rsqrt(mean_sq + 1e-06)
    out_ref[...] = (values * scale * gain_ref[...].astype(jnp.float32)).astype(out_ref.dtype)


def normalise(tokens, gain):
    return pl.pallas_call(
        norm_kernel,
        out_shape=jax.ShapeDtypeStruct(tokens.shape, tokens.dtype),
        in_specs=[pl.BlockSpec(memory_space=pltpu.VMEM)] * 2,
        out_specs=pl.BlockSpec(memory_space=pltpu.VMEM),
        name="normalise",
    )(tokens, gain)


def onward(value):
    sections = lax.axis_size("section")
    return lax.ppermute(value, "section", [(i, (i + 1) % sections) for i in range(sections)])


def local(tokens, norm_gain, w_gate, w_up, w_down, expert_ids, slot_ids, route_weight):
    row, col = lax.axis_index("row"), lax.axis_index("col")
    rows, cols = lax.axis_size("row"), lax.axis_size("col")
    count = tokens.shape[1]
    swap = [(0, 1), (1, 0)]

    named = expert_ids[0][None] == jnp.arange(EXPERTS, dtype=jnp.int32)[:, None, None]
    dense = jnp.sum(jnp.where(named, route_weight[0][None], 0.0), axis=2)
    spread = jnp.broadcast_to(dense.reshape(1, -1), (cols, EXPERTS * count))
    spread = lax.all_to_all(spread, "col", split_axis=0, concat_axis=0, tiled=True)
    spread = spread.reshape(cols, EXPERTS, count)

    normed = normalise(tokens[0], norm_gain)
    gathered = lax.all_gather(normed, "col", axis=0, tiled=True)

    gate_far = lax.ppermute(w_gate[0], "row", swap)
    up_far = lax.ppermute(w_up[0], "row", swap)
    down_far = lax.ppermute(w_down[0], "row", swap)
    first = jnp.concatenate([w_gate[0], gate_far, w_up[0], up_far], axis=1)
    second = jnp.concatenate([w_down[0], down_far], axis=0)
    first, second = lax.optimization_barrier((first, second))
    per_row = EXPERTS // rows
    mine = col // (cols // per_row)

    def weight_of(expert):
        picked = lax.dynamic_index_in_dim(spread, expert, 1, keepdims=False)
        return jnp.broadcast_to(picked.reshape(-1, 1), (cols * count, w_gate.shape[2]))

    weights = jnp.concatenate(
        [weight_of(row * per_row + mine), weight_of((1 - row) * per_row + mine)], axis=1
    )
    both = jnp.dot(gathered, first, preferred_element_type=jnp.float32)
    half = both.shape[1] // 2
    hidden = (jax.nn.silu(both[:, :half]) * both[:, half:] * weights).astype(jnp.bfloat16)
    piece = jnp.dot(hidden, second, preferred_element_type=jnp.float32).astype(jnp.bfloat16)
    summed = lax.psum_scatter(piece, "col", scatter_dimension=0, tiled=True)
    mixed = onward(tokens[0]).astype(jnp.float32) + onward(summed).astype(jnp.float32)
    return mixed.astype(jnp.bfloat16)[None]


def solution(mesh):
    sections, members = mesh.devices.shape
    fine = Mesh(mesh.devices.reshape(sections, 2, members // 2), ("section", "row", "col"))
    split = ("row", "col")
    placed = (
        P("section", split, None),
        P("section", None),
        P("section", None, split),
        P("section", None, split),
        P("section", split, None),
        P("section", split, None),
        P("section", split, None),
        P("section", split, None),
    )
    return jax.shard_map(
        local, mesh=fine, in_specs=placed, out_specs=P("section", split, None), check_vma=False
    )
```
